32 devices in a mesh: dp: 8 (over z, x), head: 4 (over y, core).
Axes of the slice: x: 2, y: 2, z: 4, core: 2. Of those that a mesh axis runs over, the one named last changes fastest.
Arguments:
- layer_in: bfloat16 [24576, 768], P(('dp', 'head')), may hold values from -6 to 6
- doc_ids: int32 [24576], P('dp'), may hold values from -1 to 16, as said below
- g_attn: bfloat16 [768], replicated, may hold values from 0.5 to 1.5
- w_qkv: bfloat16 [3, 768, 768], P(None, None, 'head'), may hold values from -0.21875 to 0.21875
- g_inner: bfloat16 [768], P('head'), may hold values from 0.5 to 1.5
- w_o: bfloat16 [768, 768], P('head'), may hold values from -0.21875 to 0.21875
- g_ffn: bfloat16 [768], replicated, may hold values from 0.5 to 1.5
- w_in: bfloat16 [3072, 768], P(('dp', 'head')), may hold values from -0.21875 to 0.21875
- g_hidden: bfloat16 [3072], P(('dp', 'head')), may hold values from 0.5 to 1.5
- w_out: bfloat16 [3072, 768], P(('dp', 'head')), may hold values from -0.109375 to 0.109375
- cotangent: bfloat16 [24576, 768], P(('dp', 'head')), may hold values from -6 to 6
Outputs:
- layer_out: bfloat16 [24576, 768], P(('dp', 'head'))
- grad_x: float32 [24576, 768], P(('dp', 'head'))
- grad_g_attn: float32 [768], replicated
- grad_w_qkv: float32 [3, 768, 768], P(None, None, 'head')
- grad_g_inner: float32 [768], P('head')
- grad_w_o: float32 [768, 768], P('head')
- grad_g_ffn: float32 [768], replicated
- grad_w_in: float32 [3072, 768], P(('dp', 'head'))
- grad_g_hidden: float32 [3072], P(('dp', 'head'))
- grad_w_out: float32 [3072, 768], P(('dp', 'head'))
The draws below stay inside these ranges and needn't reach their ends.
Inputs may be any that keep to these rules, and one draw needn't show every extreme that they name: `doc_ids`: within each group of 3072 slots, document numbers start at 0 and never fall; padding (-1) fills the end of the group, at most a quarter of it, and some group has no padding; the first document of every group has exactly 2048 tokens and none has more; every document has a multiple of 64 tokens.
All inputs are finite; a program needn't handle non-finite values.
Results may differ from the reference program's by a relative error of at most 0.015.
Values may be sent and summed in bfloat16 or wider, within the bound.
No kernel may reach another device: no remote copies, remote signals or barrier semaphores. Data moves between devices by JAX's collectives and lax.ppermute only.
A program may use at most 192 MiB of HBM per device.

```python
import jax
import jax.numpy as jnp
from jax import lax

D = 768
HEADS = 12
HEAD_DIM = 64
FF = 3072
TOK_DEV = 3072
LONGEST = 2048
TOKENS = 24576
N_DP = 8


def draw_doc_ids(key, part):
    groups = TOKENS // TOK_DEV
    unit_len = LONGEST // 32
    most_docs = TOK_DEV // unit_len
    key_len = jax.random.fold_in(key, 11)
    key_pad = jax.random.fold_in(key, 23)
    powers = jax.random.randint(key_len, (groups, most_docs), 0, 6)
    powers = powers.at[0].set(0)
    lengths = unit_len * jnp.left_shift(jnp.ones_like(powers), powers)
    lengths = lengths.at[:, 0].set(LONGEST)
    ends = jnp.cumsum(lengths, axis=1)
    position = jnp.arange(TOK_DEV, dtype=jnp.int32)
    numbers = jnp.sum((position[None, :, None] >= ends[:, None, :]).astype(jnp.int32), axis=-1)
    padding = jax.random.randint(key_pad, (groups, 1), 0, TOK_DEV // 4 + 1)
    padding = padding.at[0, 0].set(0).at[groups - 1, 0].set(TOK_DEV // 4)
    numbers = jnp.where(position[None, :] < TOK_DEV - padding, numbers, -1)
    return numbers.reshape(-1).astype(jnp.int32)


def steps_of(own_key, shape, split, smallest, high):
    factor_of = 1.0
    for axis_at, shards_of in split:
        draws = jax.random.uniform(jax.random.fold_in(jax.random.fold_in(own_key, 6), axis_at), (shards_of,), jnp.float32, smallest / len(split), high / len(split))
        factor_of = factor_of * jnp.repeat(jnp.exp(draws), shape[axis_at] // shards_of).reshape((-1,) + (1,) * (len(shape) - 1 - axis_at))
    return factor_of


def bell_draw(stream_key, extent, scale, most, shards=(), kind=jnp.bfloat16):
    result = scale * jax.random.normal(stream_key, extent, jnp.float32)
    if shards:
        result = result * steps_of(stream_key, extent, shards, -0.22, 0.18)
    return jnp.clip(result, -most, most).astype(kind)


def setup_inputs(seed: int = 0) -> dict:
    streams_of = jax.random.split(jax.random.key(seed), 12)
    layer_in = bell_draw(streams_of[0], (TOKENS, D), 1.0, 6.0, ((0, 32),))
    doc_ids = draw_doc_ids(jax.random.fold_in(streams_of[11], 71), 0)
    g_attn = jnp.clip(1.0 + 0.1 * jax.random.normal(streams_of[2], (D,), jnp.float32), 0.5, 1.5).astype(jnp.bfloat16)
    w_qkv = bell_draw(streams_of[3], (3, D, D), D ** -0.5, 0.21875, ((2, 4),))
    g_inner = jnp.clip(1.0 + 0.1 * jax.random.normal(streams_of[4], (D,), jnp.float32), 0.5, 1.5).astype(jnp.bfloat16)
    w_o = bell_draw(streams_of[5], (D, D), D ** -0.5, 0.21875, ((0, 4),))
    g_ffn = jnp.clip(1.0 + 0.1 * jax.random.normal(streams_of[6], (D,), jnp.float32), 0.5, 1.5).astype(jnp.bfloat16)
    w_in = bell_draw(streams_of[7], (FF, D), D ** -0.5, 0.21875, ((0, 32),))
    g_hidden = jnp.clip(1.0 + 0.1 * jax.random.normal(streams_of[8], (FF,), jnp.float32), 0.5, 1.5).astype(jnp.bfloat16)
    w_out = bell_draw(streams_of[9], (FF, D), FF ** -0.5, 0.109375, ((0, 32),))
    cotangent = bell_draw(streams_of[10], (TOKENS, D), 1.0, 6.0, ((0, 32),))
    return dict(layer_in=layer_in, doc_ids=doc_ids, g_attn=g_attn, w_qkv=w_qkv, g_inner=g_inner, w_o=w_o, g_ffn=g_ffn, w_in=w_in, g_hidden=g_hidden, w_out=w_out, cotangent=cotangent)


EPSILON = 1e-05
NEG_BIG = -1e+30
HIGHEST = lax.Precision.HIGHEST

@jax.custom_vjp
def low(v):
    return lax.optimization_barrier(v.astype(jnp.bfloat16)).astype(jnp.float32)

@jax.custom_vjp
def low_back(v):
    return v

def low_keep(v):
    return (low(v), None)

def low_pass(kept, grad):
    return (grad,)

def back_keep(v):
    return (v, None)

def back_low(kept, grad):
    return (low(grad),)
low.defvjp(low_keep, low_pass)
low_back.defvjp(back_keep, back_low)

def layer_norm(values, gain):
    average = lax.optimization_barrier(jnp.mean(values, axis=-1, keepdims=True))
    spread = lax.optimization_barrier(jnp.mean(values * values, axis=-1, keepdims=True)) - average * average
    return (values - average) * lax.rsqrt(spread + EPSILON) * gain

def one_group(rows_in, doc_group, g_attn, w_qkv, g_inner, w_o, g_ffn, w_in, g_hidden, w_out):
    valid = (doc_group >= 0).astype(jnp.float32)[:, None]
    start_x = rows_in * valid
    normed = low(layer_norm(start_x, g_attn))
    proj_qkv = low_back(low(jnp.einsum('td,cde->cte', normed, w_qkv, precision=HIGHEST)))
    queries = proj_qkv[0].reshape(TOK_DEV, HEADS, HEAD_DIM)
    keys = proj_qkv[1].reshape(TOK_DEV, HEADS, HEAD_DIM)
    values = proj_qkv[2].reshape(TOK_DEV, HEADS, HEAD_DIM)
    block_len = min(512, TOK_DEV)
    key_pos = jnp.arange(TOK_DEV, dtype=jnp.int32)

    def attend(offset):
        query_blk = lax.dynamic_slice_in_dim(queries, offset, block_len, 0)
        query_ids = lax.dynamic_slice_in_dim(doc_group, offset, block_len, 0)
        query_pos = offset + jnp.arange(block_len, dtype=jnp.int32)
        logits = low_back(jnp.einsum('qhd,khd->hqk', query_blk, keys, precision=HIGHEST) * HEAD_DIM ** (-0.5))
        allowed = (query_ids[:, None] == doc_group[None, :]) & (key_pos[None, :] <= query_pos[:, None])
        logits = jnp.where(allowed[None], logits, NEG_BIG)
        probs = jax.nn.softmax(logits, axis=-1)
        return jnp.einsum('hqk,khd->qhd', low(probs), values, precision=HIGHEST)
    offsets = jnp.arange(TOK_DEV // block_len, dtype=jnp.int32) * block_len
    blocks = lax.map(jax.checkpoint(attend), offsets)
    attended = low_back(blocks.reshape(TOK_DEV, D))
    normed_out = low(layer_norm(attended, g_inner))
    residual = start_x + low_back(jnp.dot(normed_out, w_o, precision=HIGHEST))
    ffn_input = low(layer_norm(residual, g_ffn))
    pre_act = low_back(jnp.dot(ffn_input, w_in.T, precision=HIGHEST))
    post_norm = low(layer_norm(jax.nn.gelu(pre_act, approximate=False), g_hidden))
    return residual + low_back(jnp.dot(post_norm, w_out, precision=HIGHEST))

def reference(layer_in, doc_ids, g_attn, w_qkv, g_inner, w_o, g_ffn, w_in, g_hidden, w_out, cotangent):
    doc_groups = doc_ids.reshape(N_DP, TOK_DEV)

    def whole_layer(inputs, gain_a, weight_qkv, gain_i, weight_o, gain_f, weight_in, gain_h, weight_out):
        stacked = inputs.reshape(N_DP, TOK_DEV, D)

        def step(carry, pieces):
            return (carry, one_group(pieces[0], pieces[1], gain_a, weight_qkv, gain_i, weight_o, gain_f, weight_in, gain_h, weight_out))
        unused, outputs = lax.scan(step, jnp.float32(0.0), (stacked, doc_groups))
        return outputs.reshape(TOKENS, D)
    params = [v.astype(jnp.float32) for v in (layer_in, g_attn, w_qkv, g_inner, w_o, g_ffn, w_in, g_hidden, w_out)]
    output, pullback = jax.vjp(whole_layer, *params)
    grads = pullback(cotangent.astype(jnp.float32))
    factor = TOKENS ** (-0.5)
    return (output.astype(jnp.bfloat16), grads[0], grads[1] * factor, grads[2] * factor, grads[3] * factor, grads[4] * factor, grads[5] * factor, grads[6] * factor, grads[7] * factor, grads[8] * factor)
```

```python
import functools
import jax, jax.numpy as jnp
from jax import lax
from jax.experimental import pallas as pl
from jax.experimental.pallas import tpu as pltpu
HEAD_DIM=64
LONGEST=2048
NEG=-1e30
C2=0.125*1.4426950408889634
bf16=jnp.bfloat16; f32=jnp.float32
NT=(((1,),(1,)),((),()))
NN=(((1,),(0,)),((),()))
TN=(((0,),(0,)),((),()))

def dg(a,b,dims): return lax.dot_general(a,b,dims,preferred_element_type=f32)

def fwd_kernel(base_ref,q_ref,k_ref,v_ref,id_ref,o_ref,lse_ref,ks,vt,acc,ms,*,nh,bq,T,BK,tmode):
    step=pl.program_id(0)
    HD=HEAD_DIM
    @pl.when(step==0)
    def _():
        for h in range(nh):
            ks[h]=k_ref[:,h*HD:(h+1)*HD]
            vv=v_ref[:,h*HD:(h+1)*HD]
            vt[h,0:HD,:]=jnp.transpose(vv.astype(f32)).astype(bf16)
            vt[h,HD:,:]=jnp.ones((vt.shape[1]-HD,T),bf16)
    qi=base_ref[0]+step
    q=[q_ref[:,h*HD:(h+1)*HD] for h in range(nh)]
    nlong=LONGEST//bq
    in2=qi>=nlong
    def blk(k0,bk,mask,first):
        for h in range(nh):
            kb=ks[h,pl.ds(k0,bk),:]
            s=dg(kb,q[h],NT)
            if mask is not None: s=jnp.where(mask,s,NEG)
            mb=jnp.max(s,axis=0,keepdims=True)
            vb=vt[h,:,pl.ds(k0,bk)]
            if first:
                mn=mb
                p=jnp.exp2(s*C2-mn*C2)
                acc[h]=dg(vb,p.astype(bf16),NN)
            else:
                mo=ms[h]
                mn=jnp.maximum(mo,mb)
                al=jnp.exp2((mo-mn)*C2)
                p=jnp.exp2(s*C2-mn*C2)
                acc[h]=acc[h]*al+dg(vb,p.astype(bf16),NN)
            ms[h]=mn
    def idcol(k0,bk):
        r=id_ref[:,pl.ds(k0,bk)].astype(f32)
        return jnp.transpose(jnp.broadcast_to(r,(8,bk)))[:,0:1]
    q0=pl.multiple_of(qi*bq,bq)
    kr=lax.broadcasted_iota(jnp.int32,(bq,bq),0)
    qc=lax.broadcasted_iota(jnp.int32,(bq,bq),1)
    idq=id_ref[:,pl.ds(q0,bq)].astype(f32)
    @pl.when(jnp.logical_not(in2))
    def _():
        blk(q0,bq,kr<=qc,True)
        per=BK//bq
        nbig=qi//per
        def body(j,_):
            blk(pl.multiple_of(j*BK,BK),BK,None,False); return 0
        lax.fori_loop(0,nbig,body,0)
        def body2(j,_):
            blk(pl.multiple_of(j*bq,bq),bq,None,False); return 0
        lax.fori_loop(nbig*per,qi,body2,0)
    @pl.when(in2)
    def _():
        blk(q0,bq,(kr<=qc)&(idcol(q0,bq)==idq),True)
        def body(j,_):
            k0=pl.multiple_of(j*bq,bq)
            blk(k0,bq,idcol(k0,bq)==idq,False); return 0
        lax.fori_loop(nlong,qi,body,0)
    for h in range(nh):
        a=acc[h]
        l=a[HD:HD+1]
        o=a[0:HD]/l
        o_ref[:,h*HD:(h+1)*HD]=jnp.transpose(o).astype(bf16)
        lse_ref[h]=ms[h]*C2+jnp.log2(l)

def attn_fwd(base,q,k,v,ids,nq,bq=256,BK=512,tmode=0):
    T,W=k.shape; nh=W//HEAD_DIM
    full=lambda shp: pl.BlockSpec(shp,lambda i,b:tuple(0 for _ in shp))
    return pl.pallas_call(
        functools.partial(fwd_kernel,nh=nh,bq=bq,T=T,BK=BK,tmode=tmode),
        grid_spec=pltpu.PrefetchScalarGridSpec(num_scalar_prefetch=1,grid=(nq,),
            in_specs=[pl.BlockSpec((bq,W),lambda i,b:(b[0]+i,0)),full((T,W)),full((T,W)),full((1,T))],
            out_specs=[pl.BlockSpec((bq,W),lambda i,b:(i,0)),pl.BlockSpec((nh,1,bq),lambda i,b:(0,0,i))],
            scratch_shapes=[pltpu.VMEM((nh,T,HEAD_DIM),bf16),pltpu.VMEM((nh,HEAD_DIM+16,T),bf16),
                            pltpu.VMEM((nh,HEAD_DIM+16,bq),f32),pltpu.VMEM((nh,1,bq),f32)]),
        out_shape=[jax.ShapeDtypeStruct((nq*bq,W),bf16),jax.ShapeDtypeStruct((nh,1,nq*bq),f32)],
        compiler_params=pltpu.CompilerParams(dimension_semantics=("arbitrary",),vmem_limit_bytes=60*2**20),
        cost_estimate=pl.CostEstimate(flops=4*nq*bq*T//3*W,bytes_accessed=4*T*W*2,transcendentals=nq*bq*T//3*nh),
        name="attn_fwd",
    )(base,q,k,v,ids)

def bwd_kernel(base_ref,q_ref,k_ref,v_ref,id_ref,go_ref,o_ref,lse_ref,dq_ref,dk_ref,dv_ref,ks,kt,vs,dka,dva,dqa,*,nh,bq,T,BK,nq):
    step=pl.program_id(0)
    HD=HEAD_DIM
    @pl.when(step==0)
    def _():
        for h in range(nh):
            kk=k_ref[:,h*HD:(h+1)*HD]
            ks[h]=kk
            kt[h]=jnp.transpose(kk.astype(f32)).astype(bf16)
            vs[h]=v_ref[:,h*HD:(h+1)*HD]
        dka[...]=jnp.zeros_like(dka)
        dva[...]=jnp.zeros_like(dva)
    qi=base_ref[0]+step
    q=[q_ref[:,h*HD:(h+1)*HD] for h in range(nh)]
    go=[go_ref[:,h*HD:(h+1)*HD] for h in range(nh)]
    gof=go_ref[...].astype(f32)*o_ref[...].astype(f32)
    gt=jnp.transpose(gof)
    delta=[jnp.sum(gt[h*HD:(h+1)*HD],axis=0,keepdims=True) for h in range(nh)]
    lse=[lse_ref[h] for h in range(nh)]
    nlong=LONGEST//bq
    in2=qi>=nlong
    def blk(k0,bk,mask,first):
        for h in range(nh):
            kb=ks[h,pl.ds(k0,bk),:]
            vb=vs[h,pl.ds(k0,bk),:]
            s=dg(kb,q[h],NT)
            if mask is not None: s=jnp.where(mask,s,NEG)
            p=jnp.exp2(s*C2-lse[h])
            dp=dg(vb,go[h],NT)
            ds=(p*(dp-delta[h])).astype(bf16)
            dva[h,pl.ds(k0,bk),:]+=dg(p.astype(bf16),go[h],NN)
            dka[h,pl.ds(k0,bk),:]+=dg(ds,q[h],NN)
            d=dg(kt[h,:,pl.ds(k0,bk)],ds,NN)
            if first: dqa[h]=d
            else: dqa[h]+=d
    def idcol(k0,bk):
        r=id_ref[:,pl.ds(k0,bk)].astype(f32)
        return jnp.transpose(jnp.broadcast_to(r,(8,bk)))[:,0:1]
    q0=pl.multiple_of(qi*bq,bq)
    kr=lax.broadcasted_iota(jnp.int32,(bq,bq),0)
    qc=lax.broadcasted_iota(jnp.int32,(bq,bq),1)
    idq=id_ref[:,pl.ds(q0,bq)].astype(f32)
    @pl.when(jnp.logical_not(in2))
    def _():
        blk(q0,bq,kr<=qc,True)
        per=BK//bq
        nbig=qi//per
        def body(j,_):
            blk(pl.multiple_of(j*BK,BK),BK,None,False); return 0
        lax.fori_loop(0,nbig,body,0)
        def body2(j,_):
            blk(pl.multiple_of(j*bq,bq),bq,None,False); return 0
        lax.fori_loop(nbig*per,qi,body2,0)
    @pl.when(in2)
    def _():
        blk(q0,bq,(kr<=qc)&(idcol(q0,bq)==idq),True)
        def body(j,_):
            k0=pl.multiple_of(j*bq,bq)
            blk(k0,bq,idcol(k0,bq)==idq,False); return 0
        lax.fori_loop(nlong,qi,body,0)
    for h in range(nh):
        dq_ref[:,h*HD:(h+1)*HD]=(jnp.transpose(dqa[h])*0.125).astype(bf16)
    @pl.when(step==nq-1)
    def _():
        for h in range(nh):
            dk_ref[:,h*HD:(h+1)*HD]=(dka[h]*0.125).astype(bf16)
            dv_ref[:,h*HD:(h+1)*HD]=dva[h].astype(bf16)

def attn_bwd(base,q,k,v,ids,go,o,lse,nq,bq=256,BK=256):
    T,W=k.shape; nh=W//HEAD_DIM; HD=HEAD_DIM
    full=lambda shp: pl.BlockSpec(shp,lambda i,b:tuple(0 for _ in shp))
    row=lambda: pl.BlockSpec((bq,W),lambda i,b:(b[0]+i,0))
    return pl.pallas_call(
        functools.partial(bwd_kernel,nh=nh,bq=bq,T=T,BK=BK,nq=nq),
        grid_spec=pltpu.PrefetchScalarGridSpec(num_scalar_prefetch=1,grid=(nq,),
            in_specs=[row(),full((T,W)),full((T,W)),full((1,T)),row(),row(),pl.BlockSpec((nh,1,bq),lambda i,b:(0,0,b[0]+i))],
            out_specs=[pl.BlockSpec((bq,W),lambda i,b:(i,0)),full((T,W)),full((T,W))],
            scratch_shapes=[pltpu.VMEM((nh,T,HD),bf16),pltpu.VMEM((nh,HD,T),bf16),pltpu.VMEM((nh,T,HD),bf16),
                            pltpu.VMEM((nh,T,HD),f32),pltpu.VMEM((nh,T,HD),f32),pltpu.VMEM((nh,HD,bq),f32)]),
        out_shape=[jax.ShapeDtypeStruct((nq*bq,W),bf16),jax.ShapeDtypeStruct((T,W),bf16),jax.ShapeDtypeStruct((T,W),bf16)],
        compiler_params=pltpu.CompilerParams(dimension_semantics=("arbitrary",),vmem_limit_bytes=60*2**20),
        cost_estimate=pl.CostEstimate(flops=10*nq*bq*T//3*W,bytes_accessed=8*T*W*2,transcendentals=nq*bq*T//3*nh),
        name="attn_bwd",
    )(base,q,k,v,ids,go,o,lse)


from jax.sharding import PartitionSpec as P

EPSILON = 1e-05


def xor_send(value, axis, bits):
    size = lax.axis_size(axis)
    return lax.ppermute(value, axis, [(i, i ^ bits) for i in range(size)])


def rows_of(value, index, count):
    return lax.dynamic_slice_in_dim(value, index * count, count, 0)


def axis_bits(axis):
    size = lax.axis_size(axis)
    return [1 << b for b in range(size.bit_length() - 1)]


def small_sum(value, axes):
    for axis in axes:
        for bits in axis_bits(axis):
            value = value + xor_send(value, axis, bits)
    return value


def halve_sum(value, axis):
    bits = [b for b in axis_bits(axis)]
    order = [bits[0]] + bits[:0:-1]
    me = lax.axis_index(axis)
    for b in order:
        half = value.shape[0] // 2
        mine = jnp.where(me & b, 1, 0)
        got = xor_send(rows_of(value, 1 - mine, half), axis, b)
        value = (rows_of(value, mine, half).astype(f32) + got.astype(f32)).astype(value.dtype)
    for b in order[::-1]:
        got = xor_send(value, axis, b)
        value = jnp.where(
            me & b, jnp.concatenate([got, value]), jnp.concatenate([value, got])
        )
    return value


def norm_stats(values, width):
    average = jnp.sum(values, axis=-1, keepdims=True) / width
    spread = jnp.sum(values * values, axis=-1, keepdims=True) / width - average * average
    return average, lax.rsqrt(spread + EPSILON)


def norm_back(err, hat, rstd, width):
    first = jnp.sum(err, axis=-1, keepdims=True) / width
    second = jnp.sum(err * hat, axis=-1, keepdims=True) / width
    return rstd * (err - first - hat * second)


def body(layer_in, doc_ids, g_attn, w_qkv, g_inner, w_o, g_ffn, w_in, g_hidden, w_out, cotangent):
    rows, width = layer_in.shape
    group_len = doc_ids.shape[0]
    local = w_qkv.shape[2]
    parts = lax.axis_size("head")
    me = lax.axis_index("head")
    hidden = w_in.shape[0] * parts * lax.axis_size("dp")
    factor = (rows * parts * lax.axis_size("dp")) ** (-0.5)
    ga, gi, gf32 = g_attn.astype(f32), g_inner.astype(f32), g_ffn.astype(f32)
    gh32 = g_hidden.astype(f32)

    own_ids = rows_of(doc_ids, me, rows)
    valid = (own_ids >= 0).astype(f32)[:, None]
    start_x = layer_in.astype(f32) * valid
    avg_a, rstd_a = norm_stats(start_x, width)
    hat_a = (start_x - avg_a) * rstd_a
    normed = (hat_a * ga).astype(bf16)
    blocks = {0: normed}
    for b in axis_bits("head")[::-1]:
        blocks.update({k ^ b: xor_send(v, "head", b) for k, v in list(blocks.items())})
    gathered = jnp.zeros((group_len, width), bf16)
    for k, v in blocks.items():
        gathered = lax.dynamic_update_slice(gathered, v, ((me ^ k) * rows, 0))

    w_o_parts = [w_o] + [xor_send(w_o, "head", k) for k in range(1, parts)]
    gi_parts = [gi] + [xor_send(gi, "head", k) for k in range(1, parts)]
    w_out_g = (w_out.astype(f32) * gh32[:, None]).astype(bf16)
    win_full = lax.all_gather(w_in, ("dp", "head"), axis=0, tiled=True)
    wout_full = lax.all_gather(w_out_g, ("dp", "head"), axis=0, tiled=True)

    qkv = jnp.einsum("td,cde->cte", gathered, w_qkv, preferred_element_type=f32).astype(bf16)
    ids_row = doc_ids[None]
    base = jnp.zeros((1,), jnp.int32)
    bq = 512
    att, lse = attn_fwd(base, qkv[0], qkv[1], qkv[2], ids_row, group_len // bq, bq=bq, BK=1024)

    att_parts = [rows_of(att, me, rows)] + [
        xor_send(rows_of(att, me ^ k, rows), "head", k) for k in range(1, parts)
    ]
    att_parts = [v.astype(f32) for v in att_parts]
    tot = sum(jnp.sum(v, axis=-1, keepdims=True) for v in att_parts)
    tot2 = sum(jnp.sum(v * v, axis=-1, keepdims=True) for v in att_parts)
    avg_i = tot / width
    rstd_i = lax.rsqrt(tot2 / width - avg_i * avg_i + EPSILON)
    hat_i = [(v - avg_i) * rstd_i for v in att_parts]
    normed_i = [(v * g).astype(bf16) for v, g in zip(hat_i, gi_parts)]
    mixed = sum(jnp.dot(v, w, preferred_element_type=f32) for v, w in zip(normed_i, w_o_parts))
    resid = start_x + mixed

    avg_f, rstd_f = norm_stats(resid, width)
    hat_f = (resid - avg_f) * rstd_f
    ffn_in = (hat_f * gf32).astype(bf16)
    pre = lax.dot_general(ffn_in, win_full, NT, preferred_element_type=f32)
    act, act_back = jax.vjp(lambda u: jax.nn.gelu(u, approximate=False), pre)
    avg_h, rstd_h = norm_stats(act, hidden)
    hat_h = (act - avg_h) * rstd_h
    hat_h16 = hat_h.astype(bf16)
    result = (resid + jnp.dot(hat_h16, wout_full, preferred_element_type=f32)).astype(bf16)

    grad_y = cotangent.astype(f32)
    d_wout = lax.dot_general(hat_h16, cotangent, TN, preferred_element_type=f32).astype(bf16)
    err_h = lax.dot_general(cotangent, wout_full, NT, preferred_element_type=f32)
    gu = act_back(norm_back(err_h, hat_h, rstd_h, hidden))[0].astype(bf16)
    d_win = lax.dot_general(gu, ffn_in, TN, preferred_element_type=f32).astype(bf16)
    g_a = jnp.dot(gu, win_full, preferred_element_type=f32)
    part_gffn = jnp.sum(g_a * hat_f, axis=0)
    g_res = grad_y + norm_back(g_a * gf32, hat_f, rstd_f, width)
    sum_wout = lax.psum_scatter(d_wout, ("dp", "head"), scatter_dimension=0, tiled=True)
    sum_win = lax.psum_scatter(d_win, ("dp", "head"), scatter_dimension=0, tiled=True)

    gz = g_res.astype(bf16)
    d_wo = [lax.dot_general(v, gz, TN, preferred_element_type=f32) for v in normed_i]
    e_i = [
        lax.dot_general(gz, w, NT, preferred_element_type=f32) * g
        for w, g in zip(w_o_parts, gi_parts)
    ]
    first = sum(jnp.sum(e, axis=-1, keepdims=True) for e in e_i) / width
    second = sum(jnp.sum(e * v, axis=-1, keepdims=True) for e, v in zip(e_i, hat_i)) / width
    g_att = [(rstd_i * (e - first - v * second)).astype(bf16) for e, v in zip(e_i, hat_i)]
    go = jnp.zeros((group_len, local), bf16)
    for k in range(parts):
        got = xor_send(g_att[k], "head", k) if k else g_att[0]
        go = lax.dynamic_update_slice(go, got, ((me ^ k) * rows, 0))
    part_wo = d_wo[0] + sum(
        xor_send(d_wo[k].astype(bf16), "head", k).astype(f32) for k in range(1, parts)
    )
    sum_wo = halve_sum(part_wo.astype(bf16), "dp").astype(f32)

    dq, dk, dv = attn_bwd(base, qkv[0], qkv[1], qkv[2], ids_row, go, att, lse, group_len // bq, bq=bq, BK=512)

    def back_rows(k):
        return sum(
            lax.dot_general(rows_of(g, me ^ k, rows), w_qkv[c], NT, preferred_element_type=f32)
            for c, g in enumerate((dq, dk, dv))
        )

    held = {k: back_rows(k).astype(bf16) for k in reversed(range(parts))}
    for b in axis_bits("head"):
        nxt = {}
        for k in sorted(held, reverse=True):
            if k & b:
                continue
            got = xor_send(held[k ^ b], "head", b)
            nxt[k] = (held[k].astype(f32) + got.astype(f32)).astype(bf16)
        held = nxt
    g_normed = held[0].astype(f32)
    d_wqkv = jnp.stack(
        [lax.dot_general(gathered, g, TN, preferred_element_type=f32) for g in (dq, dk, dv)]
    )
    part_gattn = jnp.sum(w_qkv.astype(f32) * d_wqkv, axis=(0, 2)) / ga
    sum_wqkv = halve_sum(
        d_wqkv.astype(bf16).reshape(3 * width, local), "dp"
    ).astype(f32).reshape(3, width, local)
    small = small_sum(jnp.stack([part_gattn, part_gffn]), ("head", "dp"))

    grad_in = (g_res + norm_back(g_normed * ga, hat_a, rstd_a, width)) * valid
    sum_wout = sum_wout.astype(f32)
    return (
        result,
        grad_in,
        small[0] * factor,
        sum_wqkv * factor,
        jnp.sum(w_o.astype(f32) * sum_wo, axis=-1) / gi * factor,
        sum_wo * factor,
        small[1] * factor,
        sum_win.astype(f32) * factor,
        jnp.sum(w_out.astype(f32) * sum_wout, axis=-1) * factor,
        sum_wout * gh32[:, None] * factor,
    )


def solution(mesh):
    token, feature = P(("dp", "head"), None), P(("dp", "head"))
    weight = P(None, None, "head")
    placed = (token, P("dp"), P(), weight, P("head"), P("head", None), P(), token, feature, token, token)
    given = (token, token, P(), weight, P("head"), P("head", None), P(), token, feature, token)
    return jax.shard_map(body, mesh=mesh, in_specs=placed, out_specs=given, check_vma=False)
```
